256 devices in a mesh: cfg: 2 (over core), req: 8 (over z), tok: 16 (over y, x).
Axes of the slice: x: 4, y: 4, z: 8, core: 2. Of those that a mesh axis runs over, the one named last changes fastest.
Arguments:
- image_tokens: bfloat16 [2, 8, 1024, 2432], P('cfg', 'req', 'tok')
- text_tokens: bfloat16 [2, 8, 256, 2432], P('cfg', 'req', 'tok')
- text_lengths: int32 [2, 8], P('cfg', 'req'), may hold values from 1 to 256, as said below
- modulation: float32 [2, 8, 10, 2432], P('cfg', 'req'), may hold values from -3 to 3
- latent: float32 [8, 1024, 64], P('req', 'tok', 'cfg'), may hold values from -6 to 6
- guidance: float32 [8], P('req'), may hold values from 2 to 7
- step_index: int32 [8], P('req'), may hold values from 0 to 27
- qkv_weight: bfloat16 [2432, 3, 2048], P(None, None, 'tok'), may hold values from -0.125 to 0.125
- text_kv_weight: bfloat16 [2432, 2, 2048], P(None, None, 'tok'), may hold values from -0.125 to 0.125
- query_gain: float32 [64], replicated, may hold values from 1.2 to 2.4
- key_gain: float32 [64], replicated, may hold values from 1.2 to 2.4
- text_key_gain: float32 [64], replicated, may hold values from 1.2 to 2.4
- out_weight: bfloat16 [2048, 2432], P('tok'), may hold values from -0.125 to 0.125
- up_weight: bfloat16 [2432, 9728], P(None, 'tok'), may hold values from -0.125 to 0.125
- down_weight: bfloat16 [9728, 2432], P('tok'), may hold values from -0.0625 to 0.0625
- final_weight: bfloat16 [2432, 64], replicated, may hold values from -0.125 to 0.125
Outputs:
- velocity: float32 [8, 1024, 64], P('req', 'tok', 'cfg')
- next_latent: float32 [8, 1024, 64], P('req', 'tok', 'cfg')
The draws below stay inside these ranges and needn't reach their ends.
Inputs may be any that keep to these rules, and one draw needn't show every extreme that they name: `text_lengths`: some half of some request has all 256 text slots live, and another has a single live one.
All inputs are finite; a program needn't handle non-finite values.
Results may differ from the reference program's by a relative error of at most 0.012.
Values may be sent and summed in bfloat16 or wider, within the bound.
No kernel may reach another device: no remote copies, remote signals or barrier semaphores. Data moves between devices by JAX's collectives and lax.ppermute only.
A program may use at most 128 MiB of HBM per device.

```python
import math
import jax
import jax.numpy as jnp
from jax import lax

D = 2432
HEAD = 64
FF = 9728
PATCH_OUT = 64
HEADS = 32
STEPS = 28
IMG = 1024
TXT = 256
REQ = 8
N_TOK = 16


def scaled_rows(key, shape):
    subkeys = jax.random.split(key, 3)
    row_scale = jnp.exp(jax.random.uniform(subkeys[0], shape[:-1] + (1,), jnp.float32) * math.log(10.0))
    col_scale = jnp.exp(jax.random.uniform(subkeys[1], (shape[-1],), jnp.float32) * math.log(10.0))
    noise = jax.random.normal(subkeys[2], shape, jnp.float32)
    return (noise * row_scale * col_scale * 0.125).astype(jnp.bfloat16)


def draw_image_tokens(key, part):
    return scaled_rows(jax.random.fold_in(key, 3), (2, REQ, IMG, D))


def draw_text_tokens(key, part):
    return scaled_rows(jax.random.fold_in(key, 7), (2, REQ, TXT, D))


def draw_text_lengths(key, part):
    pair_count = 2 * REQ
    lengths_drawn = jax.random.randint(jax.random.fold_in(key, 11), (pair_count,), 1, TXT + 1, jnp.int32)
    shuffled = jax.random.permutation(jax.random.fold_in(key, 13), pair_count)
    lengths_drawn = lengths_drawn.at[shuffled[0]].set(TXT).at[shuffled[1]].set(1)
    return lengths_drawn.reshape(2, REQ)


def set_ends(array, rng, smallest, high):
    spot = [jax.random.randint(jax.random.fold_in(rng, axis), (), 0, length) for axis, length in enumerate(array.shape)]
    main_axis = array.shape.index(max(array.shape))
    beside = spot[:main_axis] + [(spot[main_axis] + 1) % array.shape[main_axis]] + spot[main_axis + 1:]
    return array.at[tuple(spot)].set(smallest).at[tuple(beside)].set(high)


def levels(rng, extent, pieces, smallest, largest):
    loudness, own = 1.0, jax.random.fold_in(rng, 6)
    for position, parts in pieces:
        steps = jnp.exp(jax.random.uniform(jax.random.fold_in(own, position), (parts,), jnp.float32, smallest / len(pieces), largest / len(pieces)))
        loudness = loudness * jnp.repeat(steps, extent[position] // parts).reshape([-1 if axis == position else 1 for axis in range(len(extent))])
    return loudness


def bell_draw(stream_key, dims, scale, reach, shards=(), kind=jnp.bfloat16):
    drawn = scale * jax.random.normal(stream_key, dims, jnp.float32)
    if shards:
        drawn = drawn * levels(stream_key, dims, shards, -0.22, 0.18)
    return jnp.clip(drawn, -reach, reach).astype(kind)


def setup_inputs(seed: int = 0) -> dict:
    key_list = jax.random.split(jax.random.key(seed), 17)
    image_tokens = draw_image_tokens(jax.random.fold_in(key_list[16], 71), 0)
    text_tokens = draw_text_tokens(jax.random.fold_in(key_list[16], 71), 0)
    text_lengths = draw_text_lengths(jax.random.fold_in(key_list[16], 71), 0)
    modulation = bell_draw(key_list[3], (2, REQ, 10, D), 0.6, 3.0, ((0, 2), (1, 8)), jnp.float32)
    latent = bell_draw(key_list[4], (REQ, IMG, PATCH_OUT), 1.0, 6.0, ((0, 8), (1, 16), (2, 2)), jnp.float32)
    guidance = jnp.clip(2.0 + 5.0 * jax.random.uniform(key_list[5], (REQ,), jnp.float32) ** levels(key_list[5], (REQ,), ((0, 8),), -0.2, 0.2), 2.0, 7.0)
    step_index = set_ends(jax.random.randint(key_list[6], (REQ,), 0, STEPS), jax.random.fold_in(key_list[6], 1), 0, STEPS - 1).astype(jnp.int32)
    qkv_weight = bell_draw(key_list[7], (D, 3, HEADS * HEAD), D ** -0.5, 0.125, ((2, 16),))
    text_kv_weight = bell_draw(key_list[8], (D, 2, HEADS * HEAD), D ** -0.5, 0.125, ((2, 16),))
    query_gain = jnp.clip(jax.random.uniform(key_list[9], (HEAD,), jnp.float32, 1.2, 2.4), 1.2, 2.4)
    key_gain = jnp.clip(jax.random.uniform(key_list[10], (HEAD,), jnp.float32, 1.2, 2.4), 1.2, 2.4)
    text_key_gain = jnp.clip(jax.random.uniform(key_list[11], (HEAD,), jnp.float32, 1.2, 2.4), 1.2, 2.4)
    out_weight = bell_draw(key_list[12], (HEADS * HEAD, D), (HEADS * HEAD) ** -0.5, 0.125, ((0, 16),))
    up_weight = bell_draw(key_list[13], (D, FF), D ** -0.5, 0.125, ((1, 16),))
    down_weight = bell_draw(key_list[14], (FF, D), FF ** -0.5, 0.0625, ((0, 16),))
    final_weight = bell_draw(key_list[15], (D, PATCH_OUT), D ** -0.5, 0.125)
    return dict(image_tokens=image_tokens, text_tokens=text_tokens, text_lengths=text_lengths, modulation=modulation, latent=latent, guidance=guidance, step_index=step_index, qkv_weight=qkv_weight, text_kv_weight=text_kv_weight, query_gain=query_gain, key_gain=key_gain, text_key_gain=text_key_gain, out_weight=out_weight, up_weight=up_weight, down_weight=down_weight, final_weight=final_weight)


epsilon = 1e-06
shift_factor = 3.0

def layer_norm(values):
    row_mean = lax.optimization_barrier(jnp.mean(values, axis=-1, keepdims=True))
    centered = values - row_mean
    variance = lax.optimization_barrier(jnp.mean(centered * centered, axis=-1, keepdims=True))
    return centered * lax.rsqrt(variance + epsilon)

def modulate(values, shifts, shift_at, scale_at):
    return (layer_norm(values) * (1.0 + shifts[scale_at]) + shifts[shift_at]).astype(jnp.bfloat16)

def rms_heads(values, scaling):
    mean_square = lax.optimization_barrier(jnp.mean(values * values, axis=-1, keepdims=True))
    return values * lax.rsqrt(mean_square + epsilon) * scaling

def sigma_of(step_value):
    moment = 1.0 - step_value.astype(jnp.float32) / STEPS
    return shift_factor * moment / (1.0 + (shift_factor - 1.0) * moment)

def group_sum(columns, weight, groups):
    row_total = columns.shape[0]
    split_cols = columns.reshape(row_total, groups, -1).transpose(1, 0, 2)
    split_weight = weight.reshape(groups, -1, weight.shape[1])

    def one_group(operands):
        return jnp.dot(operands[0], operands[1], preferred_element_type=jnp.float32).astype(jnp.bfloat16)
    partials = lax.map(one_group, (split_cols, split_weight))
    return lax.optimization_barrier(jnp.sum(partials.astype(jnp.float32), axis=0))

def predict(image_rows, text_rows, live_text, shifts, qkv_weight, text_kv_weight, query_gain, key_gain, text_key_gain, out_weight, up_weight, down_weight, final_weight):
    head_cols = HEADS * HEAD
    img_in = modulate(image_rows.astype(jnp.float32), shifts, 0, 1)
    mixed = jnp.dot(img_in, qkv_weight.reshape(D, 3 * head_cols), preferred_element_type=jnp.float32).reshape(IMG, 3, HEADS, HEAD)
    query = rms_heads(mixed[:, 0], query_gain).astype(jnp.bfloat16)
    image_key = rms_heads(mixed[:, 1], key_gain).astype(jnp.bfloat16)
    image_value = mixed[:, 2].astype(jnp.bfloat16)
    txt_in = modulate(text_rows.astype(jnp.float32), shifts, 6, 7)
    text_mixed = jnp.dot(txt_in, text_kv_weight.reshape(D, 2 * head_cols), preferred_element_type=jnp.float32).reshape(TXT, 2, HEADS, HEAD)
    text_key = rms_heads(text_mixed[:, 0], text_key_gain).astype(jnp.bfloat16)
    text_value = text_mixed[:, 1].astype(jnp.bfloat16)
    keys = jnp.concatenate([image_key, text_key], axis=0)
    values_all = jnp.concatenate([image_value, text_value], axis=0)
    live_keys = jnp.arange(IMG + TXT, dtype=jnp.int32) < IMG + live_text

    def one_head(operands):
        query_head, key_head, value_head = operands
        scores = jnp.dot(query_head, key_head.T, preferred_element_type=jnp.float32) * HEAD ** (-0.5)
        weights = jnp.where(live_keys[None, :], jnp.exp(scores), 0.0)
        probabilities = (weights / lax.optimization_barrier(jnp.sum(weights, axis=1, keepdims=True))).astype(jnp.bfloat16)
        return jnp.dot(probabilities, value_head, preferred_element_type=jnp.float32).astype(jnp.bfloat16)
    heads_out = lax.map(one_head, (query.transpose(1, 0, 2), keys.transpose(1, 0, 2), values_all.transpose(1, 0, 2)))
    attention = heads_out.transpose(1, 0, 2).reshape(IMG, head_cols)
    attn_out = group_sum(attention, out_weight, N_TOK)
    first_sum = image_rows.astype(jnp.float32) + shifts[2] * attn_out
    mlp_in = modulate(first_sum, shifts, 3, 4)
    hidden = jax.nn.gelu(jnp.dot(mlp_in, up_weight, preferred_element_type=jnp.float32), approximate=True).astype(jnp.bfloat16)
    mlp_out = group_sum(hidden, down_weight, N_TOK)
    second_sum = first_sum + shifts[5] * mlp_out
    final_in = modulate(second_sum, shifts, 8, 9)
    return jnp.dot(final_in, final_weight, preferred_element_type=jnp.float32)

def reference(image_tokens, text_tokens, text_lengths, modulation, latent, guidance, step_index, qkv_weight, text_kv_weight, query_gain, key_gain, text_key_gain, out_weight, up_weight, down_weight, final_weight):

    def one_sequence(operands):
        return predict(operands[0], operands[1], operands[2], operands[3], qkv_weight, text_kv_weight, query_gain, key_gain, text_key_gain, out_weight, up_weight, down_weight, final_weight)
    predictions = lax.map(one_sequence, (image_tokens.reshape(2 * REQ, IMG, D), text_tokens.reshape(2 * REQ, TXT, D), text_lengths.reshape(2 * REQ), modulation.reshape(2 * REQ, 10, D)))
    predictions = predictions.reshape(2, REQ, IMG, PATCH_OUT)
    cond = predictions[0]
    uncond = predictions[1]
    velocity = uncond + guidance[:, None, None] * (cond - uncond)
    change = sigma_of(step_index + 1) - sigma_of(step_index)
    next_latent = latent + change[:, None, None] * velocity
    return (velocity, next_latent)
```

```python
import functools

import jax
import jax.numpy as jnp
from jax import lax
from jax.experimental import pallas as pl
from jax.experimental.pallas import tpu as pltpu
from jax.sharding import PartitionSpec as P

HEAD = 64
STEPS = 28
SIDE = 4
CUT = 1280


epsilon = 1e-06
shift_factor = 3.0


def moved(value, dy, dx):
    pairs = []
    for source in range(SIDE * SIDE):
        y, x = divmod(source, SIDE)
        pairs.append((source, (y + dy) % SIDE * SIDE + (x + dx) % SIDE))
    return lax.ppermute(value, "tok", pairs)


def swapped(value, axis, distance):
    mask = 2**distance
    pairs = [(source, source ^ mask) for source in range(lax.axis_size(axis))]
    return lax.ppermute(value, axis, pairs)


def layer_norm(values):
    row_mean = jnp.mean(values, axis=-1, keepdims=True)
    centered = values - row_mean
    variance = jnp.mean(centered * centered, axis=-1, keepdims=True)
    return centered * lax.rsqrt(variance + epsilon)


def modulate(values, shifts, shift_at, scale_at):
    return (layer_norm(values) * (1.0 + shifts[scale_at]) + shifts[shift_at]).astype(jnp.bfloat16)


def sigma_of(step_value):
    moment = 1.0 - step_value.astype(jnp.float32) / STEPS
    return shift_factor * moment / (1.0 + (shift_factor - 1.0) * moment)


def spread(parts, along_y):
    def step(payload):
        return [payload] + [
            moved(payload, d if along_y else 0, 0 if along_y else d) for d in (1, 3, 2)
        ]

    got = step(jnp.concatenate(parts, axis=0))
    return [got[0], got[1], got[3], got[2]]


def gather_rows(groups):
    sizes = [g.shape[0] for g in groups]
    edges = [sum(sizes[:i]) for i in range(len(sizes) + 1)]

    def regroup(pieces):
        return [
            jnp.concatenate([p[edges[i] : edges[i + 1]] for p in pieces], axis=0)
            for i in range(len(sizes))
        ]

    left1 = spread([g[:, :CUT] for g in groups], False)
    right1 = spread([g[:, CUT:] for g in groups], True)
    left = spread(regroup(left1), True)
    right = spread(regroup(right1), False)
    return left, right


def fold(pieces, along_y):
    total = pieces[0].astype(jnp.float32)
    for d in (1, 3, 2):
        got = moved(pieces[d], -d if along_y else 0, 0 if along_y else -d)
        total = total + got.astype(jnp.float32)
    return total


def scatter_rows(left, right, rows):
    left_sum = fold(left, True).astype(jnp.bfloat16)
    right_sum = fold(right, False).astype(jnp.bfloat16)
    left_own = fold([left_sum[i * rows : (i + 1) * rows] for i in range(SIDE)], False)
    right_own = fold([right_sum[i * rows : (i + 1) * rows] for i in range(SIDE)], True)
    return jnp.concatenate([left_own, right_own], axis=1)


def turned(values):
    rows = values.shape[0] // (SIDE * SIDE)
    return (
        values.reshape(SIDE, SIDE, rows, values.shape[1])
        .transpose(1, 0, 2, 3)
        .reshape(values.shape)
    )


def rms(values, gain):
    mean_square = jnp.mean(values * values, axis=-1, keepdims=True)
    return values * lax.rsqrt(mean_square + epsilon) * gain


def attend_kernel(blocks, mix_ref, text_ref, live_ref, gains_ref, out_ref, k_ref, v_ref, tk_ref, tv_ref):
    cols = mix_ref.shape[1] // 3
    heads = cols // HEAD

    @pl.when(pl.program_id(0) == 0)
    def _():
        for h in range(heads):
            a = h * HEAD
            k_ref[h] = rms(mix_ref[:, cols + a : cols + a + HEAD], gains_ref[1:2]).astype(jnp.bfloat16)
            v_ref[h] = mix_ref[:, 2 * cols + a : 2 * cols + a + HEAD].astype(jnp.bfloat16)
            tk_ref[h] = rms(text_ref[:, a : a + HEAD], gains_ref[2:3]).astype(jnp.bfloat16)
            tv_ref[h] = text_ref[:, cols + a : cols + a + HEAD].astype(jnp.bfloat16)

    count = mix_ref.shape[0] // blocks
    rows = pl.ds(pl.multiple_of(pl.program_id(0) * count, count), count)
    scale = HEAD**-0.5
    dims = (((1,), (1,)), ((), ()))
    for h in range(heads):
        a = h * HEAD
        q = (rms(mix_ref[rows, a : a + HEAD], gains_ref[0:1])).astype(jnp.bfloat16)
        image = jnp.exp(lax.dot_general(q, k_ref[h], dims, preferred_element_type=jnp.float32) * scale)
        text = jnp.exp(lax.dot_general(q, tk_ref[h], dims, preferred_element_type=jnp.float32) * scale)
        text = jnp.where(live_ref[...] > 0, text, 0.0)
        total = jnp.sum(image, axis=1, keepdims=True) + jnp.sum(text, axis=1, keepdims=True)
        mixed = jnp.dot(image.astype(jnp.bfloat16), v_ref[h], preferred_element_type=jnp.float32)
        mixed += jnp.dot(text.astype(jnp.bfloat16), tv_ref[h], preferred_element_type=jnp.float32)
        out_ref[:, a : a + HEAD] = (mixed / total).astype(jnp.bfloat16)


def attend(mixed, text, live, gains):
    count, cols3 = mixed.shape
    text_count = text.shape[0]
    cols = cols3 // 3
    heads = cols // HEAD
    blocks = 4
    return pl.pallas_call(
        functools.partial(attend_kernel, blocks),
        grid=(blocks,),
        in_specs=[
            pl.BlockSpec((count, cols3), lambda i: (0, 0)),
            pl.BlockSpec((text_count, 2 * cols), lambda i: (0, 0)),
            pl.BlockSpec((1, text_count), lambda i: (0, 0)),
            pl.BlockSpec((3, HEAD), lambda i: (0, 0)),
        ],
        out_specs=pl.BlockSpec((count // blocks, cols), lambda i: (i, 0)),
        out_shape=jax.ShapeDtypeStruct((count, cols), jnp.bfloat16),
        scratch_shapes=[
            pltpu.VMEM((heads, count, HEAD), jnp.bfloat16),
            pltpu.VMEM((heads, count, HEAD), jnp.bfloat16),
            pltpu.VMEM((heads, text_count, HEAD), jnp.bfloat16),
            pltpu.VMEM((heads, text_count, HEAD), jnp.bfloat16),
        ],
        compiler_params=pltpu.CompilerParams(dimension_semantics=("arbitrary",)),
        cost_estimate=pl.CostEstimate(
            flops=4 * count * (count + text_count) * cols,
            bytes_accessed=4 * count * cols3,
            transcendentals=heads * count * (count + text_count),
        ),
        name="attend",
    )(mixed, text, live, gains)


def local(
    image_tokens,
    text_tokens,
    text_lengths,
    modulation,
    latent,
    guidance,
    step_index,
    qkv_weight,
    text_kv_weight,
    query_gain,
    key_gain,
    text_key_gain,
    out_weight,
    up_weight,
    down_weight,
    final_weight,
):
    shifts = modulation[0, 0]
    own_image = image_tokens[0, 0]
    own_text = text_tokens[0, 0]
    own_count, feature_count = own_image.shape
    text_own = own_text.shape[0]
    head_cols = qkv_weight.shape[2]
    qkv_flat = qkv_weight.reshape(feature_count, 3 * head_cols)
    kv_flat = text_kv_weight.reshape(feature_count, 2 * head_cols)
    f32 = jnp.float32

    img_in = modulate(own_image.astype(f32), shifts, 0, 1)
    txt_in = modulate(own_text.astype(f32), shifts, 6, 7)
    left, right = gather_rows([img_in, txt_in])
    own4 = SIDE * own_count

    def joined(pieces, lo, hi, weight):
        return jnp.concatenate(
            [jnp.dot(p[lo:hi], weight, preferred_element_type=f32) for p in pieces], axis=0
        )

    mixed = joined(left, 0, own4, qkv_flat[:CUT]) + turned(joined(right, 0, own4, qkv_flat[CUT:]))
    text_mixed = joined(left, own4, None, kv_flat[:CUT]) + turned(
        joined(right, own4, None, kv_flat[CUT:])
    )
    me = lax.axis_index("tok")
    row = lax.iota(jnp.int32, SIDE * SIDE * text_own)
    block = row // text_own
    y = (me // SIDE - block // SIDE + SIDE) % SIDE
    x = (me % SIDE - block % SIDE + SIDE) % SIDE
    slot = (y * SIDE + x) * text_own + row % text_own
    live = (slot < text_lengths[0, 0]).astype(f32)[None]
    gains = jnp.stack([query_gain, key_gain, text_key_gain])
    attention = attend(mixed, text_mixed, live, gains)

    def terms(values, weight):
        other = turned(values)
        left = [
            jnp.dot(values[i * own4 : (i + 1) * own4], weight[:, :CUT], preferred_element_type=f32).astype(jnp.bfloat16)
            for i in range(SIDE)
        ]
        right = [
            jnp.dot(other[i * own4 : (i + 1) * own4], weight[:, CUT:], preferred_element_type=f32).astype(jnp.bfloat16)
            for i in range(SIDE)
        ]
        return left, right

    summed = scatter_rows(*terms(attention, out_weight), own_count)
    residual = own_image.astype(f32) + shifts[2] * summed
    left, right = gather_rows([modulate(residual, shifts, 3, 4)])
    before = joined(left, 0, None, up_weight[:CUT]) + turned(joined(right, 0, None, up_weight[CUT:]))
    hidden = jax.nn.gelu(before, approximate=True).astype(jnp.bfloat16)
    summed = scatter_rows(*terms(hidden, down_weight), own_count)
    second_sum = residual + shifts[5] * summed
    final_in = modulate(second_sum, shifts, 8, 9)
    prediction = jnp.dot(final_in, final_weight, preferred_element_type=f32)
    channel_half = prediction.shape[1] // 2
    half_index = lax.axis_index("cfg")
    kept = lax.dynamic_slice_in_dim(prediction, half_index * channel_half, channel_half, 1)
    given = lax.dynamic_slice_in_dim(prediction, (1 - half_index) * channel_half, channel_half, 1)
    partner = swapped(given, "cfg", 0)
    first_half = half_index == 0
    cond = jnp.where(first_half, kept, partner)
    uncond = jnp.where(first_half, partner, kept)
    velocity = uncond + guidance[0] * (cond - uncond)
    change = sigma_of(step_index[0] + 1) - sigma_of(step_index[0])
    next_latent = latent[0] + change * velocity
    return (velocity[None], next_latent[None])


def solution(mesh):
    placed = (
        P("cfg", "req", "tok", None),
        P("cfg", "req", "tok", None),
        P("cfg", "req"),
        P("cfg", "req", None, None),
        P("req", "tok", "cfg"),
        P("req"),
        P("req"),
        P(None, None, "tok"),
        P(None, None, "tok"),
        P(),
        P(),
        P(),
        P("tok", None),
        P(None, "tok"),
        P("tok", None),
        P(),
    )
    return jax.shard_map(
        local,
        mesh=mesh,
        in_specs=placed,
        out_specs=(P("req", "tok", "cfg"), P("req", "tok", "cfg")),
        check_vma=False,
    )
```

```python
import functools

import jax
import jax.numpy as jnp
from jax import lax
from jax.experimental import pallas as pl
from jax.experimental.pallas import tpu as pltpu
from jax.sharding import PartitionSpec as P

HEAD = 64
STEPS = 28
SIDE = 4
CUT = 1280


epsilon = 1e-06
shift_factor = 3.0


def moved(value, dy, dx):
    pairs = []
    for source in range(SIDE * SIDE):
        y, x = divmod(source, SIDE)
        pairs.append((source, (y + dy) % SIDE * SIDE + (x + dx) % SIDE))
    return lax.ppermute(value, "tok", pairs)


def swapped(value, axis, distance):
    mask = 2**distance
    pairs = [(source, source ^ mask) for source in range(lax.axis_size(axis))]
    return lax.ppermute(value, axis, pairs)


def layer_norm(values):
    row_mean = jnp.mean(values, axis=-1, keepdims=True)
    centered = values - row_mean
    variance = jnp.mean(centered * centered, axis=-1, keepdims=True)
    return centered * lax.rsqrt(variance + epsilon)


def modulate(values, shifts, shift_at, scale_at):
    return (layer_norm(values) * (1.0 + shifts[scale_at]) + shifts[shift_at]).astype(jnp.bfloat16)


def sigma_of(step_value):
    moment = 1.0 - step_value.astype(jnp.float32) / STEPS
    return shift_factor * moment / (1.0 + (shift_factor - 1.0) * moment)


def spread(payload, along_y):
    got = [payload] + [moved(payload, d if along_y else 0, 0 if along_y else d) for d in (1, 3, 2)]
    return [got[0], got[1], got[3], got[2]]


def gather_rows(left, right):
    left1 = jnp.concatenate(spread(left, False), axis=0)
    right1 = jnp.concatenate(spread(right, True), axis=0)
    return spread(left1, True), spread(right1, False)


def fold(pieces, along_y):
    total = pieces[0].astype(jnp.float32)
    for d in (1, 3, 2):
        got = moved(pieces[d], -d if along_y else 0, 0 if along_y else -d)
        total = total + got.astype(jnp.float32)
    return total


def scatter_rows(left, right, rows):
    left_sum = fold(left, True).astype(jnp.bfloat16)
    right_sum = fold(right, False).astype(jnp.bfloat16)
    left_own = fold([left_sum[i * rows : (i + 1) * rows] for i in range(SIDE)], False)
    right_own = fold([right_sum[i * rows : (i + 1) * rows] for i in range(SIDE)], True)
    return jnp.concatenate([left_own, right_own], axis=1)


VMEM = pl.BlockSpec(memory_space=pltpu.VMEM)


def enter_kernel(image_ref, text_ref, shifts_ref, left_ref, right_ref):
    def put(rows, values, shift_at, scale_at):
        scale = 1.0 + shifts_ref[scale_at : scale_at + 1]
        ready = (layer_norm(values.astype(jnp.float32)) * scale + shifts_ref[shift_at : shift_at + 1]).astype(jnp.bfloat16)
        left_ref[rows] = ready[:, :CUT]
        right_ref[rows] = ready[:, CUT:]

    own = image_ref.shape[0]
    put(slice(0, own), image_ref[...], 0, 1)
    put(slice(own, own + text_ref.shape[0]), text_ref[...], 6, 7)


def enter(image, text, shifts):
    rows = image.shape[0] + text.shape[0]
    return pl.pallas_call(
        enter_kernel,
        in_specs=[VMEM] * 3,
        out_specs=[VMEM] * 2,
        out_shape=[
            jax.ShapeDtypeStruct((rows, CUT), jnp.bfloat16),
            jax.ShapeDtypeStruct((rows, image.shape[1] - CUT), jnp.bfloat16),
        ],
        name="enter",
    )(image, text, shifts)


def rms(values, gain):
    mean_square = jnp.mean(values * values, axis=-1, keepdims=True)
    return values * lax.rsqrt(mean_square + epsilon) * gain


def assemble(lefts, rights, target, first, count, stride, at):
    for dy in range(SIDE):
        for dx in range(SIDE):
            rows = slice(at + (dy * SIDE + dx) * count, at + (dy * SIDE + dx + 1) * count)
            target[rows, :CUT] = lefts[dy][dx * stride + first : dx * stride + first + count]
            target[rows, CUT:] = rights[dx][dy * stride + first : dy * stride + first + count]


def attend_kernel(own, own_text, *refs):
    lefts, rights = refs[:4], refs[4:8]
    qkv_ref, kv_ref, live_ref, gains_ref, out_ref, turned_ref, x_ref, w_ref, q_ref, k_ref, v_ref = refs[8:]
    bf16, f32 = jnp.bfloat16, jnp.float32
    blocks = SIDE * SIDE
    count, text_count = own * blocks, own_text * blocks
    stride = own + own_text
    assemble(lefts, rights, x_ref, 0, own, stride, 0)
    assemble(lefts, rights, x_ref, own, own_text, stride, count)
    cols = qkv_ref.shape[2]
    heads = cols // HEAD
    for p in range(3):
        w_ref[:, p * cols : (p + 1) * cols] = qkv_ref[p]
    step = count // SIDE

    def project(i, _):
        rows = pl.ds(pl.multiple_of(i * step, step), step)
        mixed = jnp.dot(x_ref[rows, :], w_ref[...], preferred_element_type=f32)
        for h in range(heads):
            a = h * HEAD
            q_ref[h, rows, :] = rms(mixed[:, a : a + HEAD], gains_ref[0:1]).astype(bf16)
            k_ref[h, rows, :] = rms(mixed[:, cols + a : cols + a + HEAD], gains_ref[1:2]).astype(bf16)
            v_ref[h, rows, :] = mixed[:, 2 * cols + a : 2 * cols + a + HEAD].astype(bf16)
        return 0

    lax.fori_loop(0, SIDE, project, 0)
    text_rows = slice(count, count + text_count)
    mixed = jnp.dot(x_ref[text_rows, :], kv_ref[...], preferred_element_type=f32)
    for h in range(heads):
        a = h * HEAD
        k_ref[h, text_rows, :] = rms(mixed[:, a : a + HEAD], gains_ref[2:3]).astype(bf16)
        v_ref[h, text_rows, :] = mixed[:, cols + a : cols + a + HEAD].astype(bf16)
    scale = HEAD**-0.5
    dims = (((1,), (1,)), ((), ()))

    def block(i, _):
        rows = pl.ds(pl.multiple_of(i * step, step), step)
        outs = []
        for h in range(heads):
            q = q_ref[h, rows, :]
            image = jnp.exp(lax.dot_general(q, k_ref[h, :count, :], dims, preferred_element_type=f32) * scale)
            text = jnp.exp(lax.dot_general(q, k_ref[h, text_rows, :], dims, preferred_element_type=f32) * scale)
            text = jnp.where(live_ref[...] > 0, text, 0.0)
            total = jnp.sum(image, axis=1, keepdims=True) + jnp.sum(text, axis=1, keepdims=True)
            mix = jnp.dot(image.astype(bf16), v_ref[h, :count, :], preferred_element_type=f32)
            mix += jnp.dot(text.astype(bf16), v_ref[h, text_rows, :], preferred_element_type=f32)
            outs.append((mix / total).astype(bf16))
        out = jnp.concatenate(outs, axis=1)
        out_ref[rows, :] = out
        for dx in range(SIDE):
            turned_ref[pl.ds(pl.multiple_of(dx * step + i * own, own), own), :] = out[dx * own : (dx + 1) * own]
        return 0

    lax.fori_loop(0, SIDE, block, 0)


def attend(lefts, rights, qkv, kv, live, gains, own, own_text):
    cols = qkv.shape[2]
    heads = cols // HEAD
    blocks = SIDE * SIDE
    count, total = own * blocks, (own + own_text) * blocks
    width = qkv.shape[1]
    out = jax.ShapeDtypeStruct((count, cols), jnp.bfloat16)
    return pl.pallas_call(
        functools.partial(attend_kernel, own, own_text),
        in_specs=[VMEM] * 12,
        out_specs=[VMEM] * 2,
        out_shape=[out, out],
        scratch_shapes=[
            pltpu.VMEM((total, width), jnp.bfloat16),
            pltpu.VMEM((width, 3 * cols), jnp.bfloat16),
            pltpu.VMEM((heads, count, HEAD), jnp.bfloat16),
            pltpu.VMEM((heads, total, HEAD), jnp.bfloat16),
            pltpu.VMEM((heads, total, HEAD), jnp.bfloat16),
        ],
        cost_estimate=pl.CostEstimate(
            flops=4 * count * total * cols + 6 * count * width * cols,
            bytes_accessed=4 * total * width,
            transcendentals=heads * count * total,
        ),
        name="attend",
    )(*lefts, *rights, qkv, kv, live, gains)


def expand_kernel(own, *refs):
    lefts, rights = refs[:4], refs[4:8]
    up_ref, out_ref, turned_ref, x_ref = refs[8:]
    assemble(lefts, rights, x_ref, 0, own, own, 0)
    step = SIDE * own
    dims = (((1,), (1,)), ((), ()))

    def block(i, _):
        rows = pl.ds(pl.multiple_of(i * step, step), step)
        before = lax.dot_general(x_ref[rows, :], up_ref[...], dims, preferred_element_type=jnp.float32)
        out = jax.nn.gelu(before, approximate=True).astype(jnp.bfloat16)
        out_ref[rows, :] = out
        for dx in range(SIDE):
            turned_ref[pl.ds(pl.multiple_of(dx * step + i * own, own), own), :] = out[dx * own : (dx + 1) * own]
        return 0

    lax.fori_loop(0, SIDE, block, 0)


def expand(lefts, rights, up_turned, own):
    units, width = up_turned.shape
    count = own * SIDE * SIDE
    out = jax.ShapeDtypeStruct((count, units), jnp.bfloat16)
    return pl.pallas_call(
        functools.partial(expand_kernel, own),
        in_specs=[VMEM] * 9,
        out_specs=[VMEM] * 2,
        out_shape=[out, out],
        scratch_shapes=[pltpu.VMEM((count, width), jnp.bfloat16)],
        cost_estimate=pl.CostEstimate(
            flops=2 * count * units * width, bytes_accessed=4 * count * width, transcendentals=count * units
        ),
        name="expand",
    )(*lefts, *rights, up_turned)


def local(
    image_tokens,
    text_tokens,
    text_lengths,
    modulation,
    latent,
    guidance,
    step_index,
    qkv_weight,
    text_kv_weight,
    query_gain,
    key_gain,
    text_key_gain,
    out_weight,
    up_weight,
    down_weight,
    final_weight,
):
    shifts = modulation[0, 0]
    own_image = image_tokens[0, 0]
    own_text = text_tokens[0, 0]
    own_count, feature_count = own_image.shape
    text_own = own_text.shape[0]
    head_cols = qkv_weight.shape[2]
    kv_flat = text_kv_weight.reshape(feature_count, 2 * head_cols)
    f32 = jnp.float32
    own4 = SIDE * own_count

    left, right = gather_rows(*enter(own_image, own_text, shifts))
    me = lax.axis_index("tok")
    row = lax.iota(jnp.int32, SIDE * SIDE * text_own)
    block = row // text_own
    y = (me // SIDE - block // SIDE + SIDE) % SIDE
    x = (me % SIDE - block % SIDE + SIDE) % SIDE
    slot = (y * SIDE + x) * text_own + row % text_own
    live = (slot < text_lengths[0, 0]).astype(f32)[None]
    gains = jnp.stack([query_gain, key_gain, text_key_gain])
    attention = attend(
        left, right, qkv_weight.transpose(1, 0, 2), kv_flat, live, gains, own_count, text_own
    )

    def terms(values, other, weight):
        def pieces(source, lo, hi):
            return [
                jnp.dot(
                    source[i * own4 : (i + 1) * own4], weight[:, lo:hi], preferred_element_type=f32
                ).astype(jnp.bfloat16)
                for i in range(SIDE)
            ]

        return pieces(values, 0, CUT), pieces(other, CUT, None)

    summed = scatter_rows(*terms(*attention, out_weight), own_count)
    residual = own_image.astype(f32) + shifts[2] * summed
    mlp_in = modulate(residual, shifts, 3, 4)
    left, right = gather_rows(mlp_in[:, :CUT], mlp_in[:, CUT:])
    hidden = expand(left, right, up_weight.T, own_count)
    summed = scatter_rows(*terms(*hidden, down_weight), own_count)
    second_sum = residual + shifts[5] * summed
    final_in = modulate(second_sum, shifts, 8, 9)
    prediction = jnp.dot(final_in, final_weight, preferred_element_type=f32)
    channel_half = prediction.shape[1] // 2
    half_index = lax.axis_index("cfg")
    kept = lax.dynamic_slice_in_dim(prediction, half_index * channel_half, channel_half, 1)
    given = lax.dynamic_slice_in_dim(prediction, (1 - half_index) * channel_half, channel_half, 1)
    partner = swapped(given, "cfg", 0)
    first_half = half_index == 0
    cond = jnp.where(first_half, kept, partner)
    uncond = jnp.where(first_half, partner, kept)
    velocity = uncond + guidance[0] * (cond - uncond)
    change = sigma_of(step_index[0] + 1) - sigma_of(step_index[0])
    next_latent = latent[0] + change * velocity
    return (velocity[None], next_latent[None])


def solution(mesh):
    placed = (
        P("cfg", "req", "tok", None),
        P("cfg", "req", "tok", None),
        P("cfg", "req"),
        P("cfg", "req", None, None),
        P("req", "tok", "cfg"),
        P("req"),
        P("req"),
        P(None, None, "tok"),
        P(None, None, "tok"),
        P(),
        P(),
        P(),
        P("tok", None),
        P(None, "tok"),
        P("tok", None),
        P(),
    )
    return jax.shard_map(
        local,
        mesh=mesh,
        in_specs=placed,
        out_specs=(P("req", "tok", "cfg"), P("req", "tok", "cfg")),
        check_vma=False,
    )
```
